32 devices in a mesh: parts: 2 (over x), expert: 16 (over z, y, core).
Axes of the slice: x: 2, y: 2, z: 4, core: 2. Of those that a mesh axis runs over, the one named last changes fastest.
Arguments:
- tokens: bfloat16 [2, 128, 7168], P(None, ('parts', 'expert')), parts along dimension 1, may hold values from -6 to 6
- live_rows: int32 [2, 32], P(None, ('parts', 'expert')), parts along dimension 1, may hold values from 3 to 4
- expert_ids: int32 [1, 2, 128, 8], P(None, None, ('parts', 'expert')), parts along dimension 2, may hold values from 0 to 15, all different within a row; in each aligned block of 4 rows (0 to 3, 4 to 7, ..., all dimensions but the last counted through in order) at most 2 rows name the same one
- gate_weights: float32 [1, 2, 128, 8], P(None, None, ('parts', 'expert')), parts along dimension 2, may hold values from 0.25 to 2.5
- norm_gain: float32 [1, 7168], replicated, may hold values from 0.1 to 1.9
- expert_gate_up: bfloat16 [1, 16, 7168, 2048], P(None, 'expert'), may hold values from -0.0625 to 0.0625
- expert_down: bfloat16 [1, 16, 1024, 7168], P(None, 'expert'), may hold values from -0.1875 to 0.1875
- shared_gate_up: bfloat16 [1, 7168, 2048], P(None, 'expert'), may hold values from -0.0625 to 0.0625
- shared_down: bfloat16 [1, 1024, 7168], P(None, None, 'expert'), may hold values from -0.1875 to 0.1875
Outputs:
- hidden_out: bfloat16 [2, 128, 7168], P(None, ('parts', 'expert')), parts along dimension 1
The draws below stay inside these ranges and needn't reach their ends.
There are 2 independent parts, one for each index of `parts`. The reference program is written for one: setup_inputs(seed, part) draws one part's arguments, and reference() takes and returns one part's arrays. A program takes and returns all parts, laid end to end along the dimension named above; an argument that names none is the same for every part. Nothing has to cross between parts.
Inputs may be any that keep to these rules, and one draw needn't show every extreme that they name: `expert_ids`: the 8 ids of a row differ; within the rows of one device for one layer and step, no expert is named by more than 2 rows, a bound that some block reaches.
All inputs are finite; a program needn't handle non-finite values.
Results may differ from the reference program's by a relative error of at most 0.0068.
Values may be sent and summed in bfloat16 or wider, within the bound.
No kernel may reach another device: no remote copies, remote signals or barrier semaphores. Data moves between devices by JAX's collectives and lax.ppermute only.
A program may use at most 128 MiB of HBM per device.

```python
import math
import jax
import jax.numpy as jnp
import numpy as np
from jax import lax

D = 7168
TOP = 8
HID = 1024
SHARED = 1024
EXPERTS = 16
LAYERS = 1
STEPS = 2
ROWS_DEV = 4
GROUP = 1
TOKENS = 64
CAP = 2
N_EXPERT = 16


def with_ends(values, own_key, least, top_value):
    index_at = [jax.random.randint(jax.random.fold_in(own_key, axis), (), 0, length) for axis, length in enumerate(values.shape)]
    longest = values.shape.index(max(values.shape))
    beside = index_at[:longest] + [(index_at[longest] + 1) % values.shape[longest]] + index_at[longest + 1:]
    return values.at[tuple(index_at)].set(least).at[tuple(beside)].set(top_value)


def levels(own_key, shape, shards, low, top_value):
    gain, own = 1.0, jax.random.fold_in(own_key, 6)
    for axis_at, shards_of in shards:
        heights = jnp.exp(jax.random.uniform(jax.random.fold_in(own, axis_at), (shards_of,), jnp.float32, low / len(shards), top_value / len(shards)))
        gain = gain * jnp.repeat(heights, shape[axis_at] // shards_of).reshape([-1 if axis == axis_at else 1 for axis in range(len(shape))])
    return gain


def deal_out(stream_key, own, number, rows, number_of, top, most, lean):
    sequence = jax.random.permutation(stream_key, number_of)
    packed, common = shares(number_of, rows * top, most, lean, True), shares(number_of, rows * top, most, lean, False)
    places = jnp.arange(number_of)

    def named(sizes, rotation):
        used = int((sizes > 0).sum())
        fixed = max(1, used // 4)
        shifted = fixed + (places - fixed + rotation * (used - fixed)) % max(1, number_of - fixed)
        return jnp.zeros((number_of,), jnp.int32).at[sequence[jnp.where(places < fixed, places, shifted)]].set(jnp.asarray(sizes, jnp.int32))

    sizes = jnp.where(number % 4 == 0, named(packed, number // 4), named(common, number - number // 4 - 1))
    mixed = jax.random.permutation(jax.random.fold_in(own, 3), number_of)
    donor, taker = mixed[0:number_of // 2 * 2:2], mixed[1:number_of // 2 * 2:2]
    room = jnp.minimum(sizes[donor] - 1, most - sizes[taker]) // 2
    room = jnp.where((donor == sequence[0]) | (taker == sequence[0]) | (sizes[taker] == 0), 0, jnp.maximum(room, 0))
    shifted = jax.random.randint(jax.random.fold_in(own, 4), (number_of // 2,), 0, 1 << 20) % (room + 1)
    sizes = sizes.at[donor].add(-shifted).at[taker].add(shifted)
    items = jnp.searchsorted(jnp.cumsum(sizes), jnp.arange(rows * top), side="right").astype(jnp.int32)
    table = items.reshape(top, rows).T
    table = table[jax.random.permutation(jax.random.fold_in(own, 1), rows)]
    rotation = jax.random.randint(jax.random.fold_in(own, 2), (rows, 1), 0, top)
    return jnp.take_along_axis(table, (jnp.arange(top)[None, :] + rotation) % top, axis=1)


def shares(count, total, most, lean, full):
    loads = [(1 << 20) // math.isqrt(rank ** lean) + 1 for rank in range(1, count + 1)]
    largest = most if full else min(most, max(-(-total // count), total * loads[0] // sum(loads)))
    least = 1 if total - largest >= count - 1 else 0
    given, surplus = [largest] + [least] * (count - 1), total - largest - least * (count - 1)
    while surplus > 0:
        candidates = [i for i in range(1, count) if given[i] < largest] or [i for i in range(1, count) if given[i] < most]
        mass, left = sum([loads[i] for i in candidates]), surplus
        for i in candidates:
            more = min(most - given[i], max(1, left * loads[i] // mass), surplus)
            given[i] = given[i] + more
            surplus = surplus - more
    return np.array(given)


def centred(key, extent, spread, bound, shards=(), held_as=jnp.bfloat16):
    entries = spread * jax.random.normal(key, extent, jnp.float32)
    if shards:
        entries = entries * levels(key, extent, shards, -0.22, 0.18)
    return jnp.clip(entries, -bound, bound).astype(held_as)


def setup_inputs(seed: int = 0, part: int = 0) -> dict:
    arg_keys = jax.random.split(jax.random.key(seed), 10)
    part_splits = jax.random.split(jax.random.fold_in(arg_keys[9], part), 10)
    tokens = centred(part_splits[0], (STEPS, TOKENS, D), 1.0, 6.0, ((1, 16),))
    live_rows = with_ends(jax.random.randint(part_splits[1], (STEPS, N_EXPERT), (3 * ROWS_DEV) // 4, ROWS_DEV + 1), jax.random.fold_in(part_splits[1], 1), (3 * ROWS_DEV) // 4, ROWS_DEV).astype(jnp.int32)
    expert_ids_keys = jax.random.split(jax.random.fold_in(part_splits[2], 1), LAYERS * STEPS * TOKENS // ROWS_DEV)
    expert_ids_turns = jax.random.permutation(jax.random.fold_in(part_splits[2], 3), LAYERS * STEPS * TOKENS // ROWS_DEV)
    expert_ids = jax.vmap(lambda own, number: deal_out(jax.random.fold_in(part_splits[2], 2), own, number, ROWS_DEV, EXPERTS, TOP, CAP, 2))(expert_ids_keys, expert_ids_turns).reshape((LAYERS, STEPS, TOKENS, TOP))
    gate_weights = jnp.clip(jnp.exp(math.log(2.5) - 2.3025851 * jax.random.uniform(part_splits[3], (LAYERS, STEPS, TOKENS, TOP), jnp.float32) ** levels(part_splits[3], (LAYERS, STEPS, TOKENS, TOP), ((2, 16),), -0.2, 0.2)), 0.25, 2.5)
    norm_gain = jnp.clip(1.0 + 0.18 * jax.random.normal(arg_keys[4], (LAYERS, D), jnp.float32), 0.1, 1.9)
    expert_gate_up = centred(arg_keys[5], (LAYERS, EXPERTS * GROUP, D, 2 * HID // GROUP), D ** -0.5, 0.0625, ((1, 16),))
    expert_down = centred(arg_keys[6], (LAYERS, EXPERTS * GROUP, HID // GROUP, D), HID ** -0.5, 0.1875, ((1, 16),))
    shared_gate_up = centred(arg_keys[7], (LAYERS, D, 2 * SHARED), D ** -0.5, 0.0625, ((1, 16),))
    shared_down = centred(arg_keys[8], (LAYERS, SHARED, D), SHARED ** -0.5, 0.1875, ((2, 16),))
    return {"tokens": tokens, "live_rows": live_rows, "expert_ids": expert_ids, "gate_weights": gate_weights, "norm_gain": norm_gain, "expert_gate_up": expert_gate_up, "expert_down": expert_down, "shared_gate_up": shared_gate_up, "shared_down": shared_down}


EPSILON = 1e-06

def rms_normed(hidden, gain_row):
    widened = hidden.astype(jnp.float32)
    scaling = lax.rsqrt(lax.optimization_barrier(jnp.mean(widened * widened, axis=-1, keepdims=True)) + EPSILON)
    return (widened * scaling * gain_row).astype(jnp.bfloat16)

def swiglu(inputs, gate_up, down_proj, unit_count):
    projected = jnp.dot(inputs, gate_up, preferred_element_type=jnp.float32)
    activated = (jax.nn.silu(projected[:, :unit_count]) * projected[:, unit_count:]).astype(jnp.bfloat16)
    return jnp.dot(activated, down_proj, preferred_element_type=jnp.float32).astype(jnp.bfloat16)

def partial_swiglu(inputs, gate_up, down_proj, unit_count):
    projected = jnp.dot(inputs, gate_up, preferred_element_type=jnp.float32)
    activated = (jax.nn.silu(projected[:, :unit_count]) * projected[:, unit_count:]).astype(jnp.bfloat16)
    return jnp.dot(activated, down_proj, preferred_element_type=jnp.float32)

def routed_sum(normed, id_block, gate_block, is_live, gate_up, down_proj):
    unit_block = HID // GROUP
    grouped_up = gate_up.reshape(EXPERTS, GROUP, D, 2 * unit_block)
    grouped_down = down_proj.reshape(EXPERTS, GROUP, unit_block, D)
    flat_ids = jnp.where(is_live[:, None], id_block, -1).reshape(-1)
    flat_gates = gate_block.reshape(-1)
    slot_count = N_EXPERT * CAP

    def one_expert(carry_sum, expert):
        hit_mask = (flat_ids == expert).astype(jnp.int32)
        ordering = jnp.argsort(-hit_mask, stable=True)[:slot_count]
        picked = hit_mask[ordering].astype(jnp.float32)
        row_index = (ordering // TOP).astype(jnp.int32)
        chosen = normed[row_index]
        upper = grouped_up[expert]
        lower = grouped_down[expert]
        total = jnp.zeros((slot_count, D), jnp.float32)
        for member in range(GROUP):
            total = total + partial_swiglu(chosen, upper[member], lower[member], unit_block)
        outputs = total.astype(jnp.bfloat16)
        weighted = (flat_gates[ordering] * picked)[:, None] * outputs.astype(jnp.float32)
        return (carry_sum.at[row_index].add(weighted), None)
    start_sum = jnp.zeros((TOKENS, D), jnp.float32)
    final_sum, _ = lax.scan(one_expert, start_sum, jnp.arange(EXPERTS, dtype=jnp.int32))
    return final_sum

def reference(tokens, live_rows, expert_ids, gate_weights, norm_gain, expert_gate_up, expert_down, shared_gate_up, shared_down):
    position = jnp.arange(TOKENS, dtype=jnp.int32)
    results = []
    for step_at in range(STEPS):
        is_live = position % ROWS_DEV < jnp.repeat(live_rows[step_at], ROWS_DEV)
        hidden = tokens[step_at]
        for layer_at in range(LAYERS):
            normed = rms_normed(hidden, norm_gain[layer_at])
            combined = routed_sum(normed, expert_ids[layer_at, step_at], gate_weights[layer_at, step_at], is_live, expert_gate_up[layer_at], expert_down[layer_at])
            shared = swiglu(normed, shared_gate_up[layer_at], shared_down[layer_at], SHARED)
            combined = combined + shared.astype(jnp.float32)
            hidden = (hidden.astype(jnp.float32) + jnp.where(is_live[:, None], combined, 0.0)).astype(jnp.bfloat16)
        results.append(hidden)
    return jnp.stack(results)
```

```python
import functools

import jax
import jax.numpy as jnp
from jax import lax
from jax.experimental import pallas as pl
from jax.experimental.pallas import tpu as pltpu
from jax.sharding import PartitionSpec as P

EXPERTS = 16
EPSILON = 1e-06
LANES = 128
COLUMN_PARTS = 2
SMALL_GRANT = 8 << 20
ROUTED_GRANT = 18 << 20
UP_STEP, UP_SLOTS = 512, 3
DOWN_STEP, DOWN_SLOTS = 896, 3


F32 = jnp.float32
BF16 = jnp.bfloat16


def vmem_spec():
    return pl.BlockSpec(memory_space=pltpu.VMEM)


def any_spec():
    return pl.BlockSpec(memory_space=pl.ANY)


def hbm_spec():
    return pl.BlockSpec(memory_space=pltpu.HBM)


def in_hbm(value):
    return pltpu.with_memory_space_constraint(value, pltpu.HBM)


def small_grant():
    return pltpu.CompilerParams(vmem_limit_bytes=SMALL_GRANT)


def largest_step(total, unit, limit):
    best = None
    for step in range(unit, limit + 1, unit):
        if total % step == 0:
            best = step
    return best if best is not None else total


def payload_kernel(expert_count, *refs):
    inputs, rest = refs[:5], refs[5:]
    near, sems, outs = rest[-6:-1], rest[-1], rest[:-6]
    copies = [pltpu.make_async_copy(inputs[at], near[at], sems.at[at]) for at in range(5)]
    for copy in copies:
        copy.start()
    for copy in copies:
        copy.wait()
    live_ref, tokens_ref, ids_ref, gates_ref, gain_ref = near
    out_ref, shares = outs[0], outs[1:]
    step_count, row_count, width = tokens_ref.shape
    top_count = ids_ref.shape[3]
    lane = lax.broadcasted_iota(jnp.int32, (row_count, LANES), 1)
    position = lax.broadcasted_iota(jnp.int32, (row_count, LANES), 0)
    third = jnp.where(lane >= 2 * expert_count, 2, jnp.where(lane >= expert_count, 1, 0))
    named = lane - third * expert_count
    for step_at in range(step_count):
        rows = pl.ds(step_at * row_count, row_count)
        widened = tokens_ref[step_at].astype(F32)
        scaling = lax.rsqrt(jnp.sum(widened * widened, axis=-1, keepdims=True) / width + EPSILON)
        out_ref[rows, pl.ds(0, width)] = (widened * scaling * gain_ref[...]).astype(BF16)
        table = jnp.zeros((row_count, LANES), F32)
        for k in range(top_count):
            chosen = ids_ref[0, step_at, :, k : k + 1]
            gate = gates_ref[0, step_at, :, k : k + 1]
            table = table + jnp.where(named == chosen, gate, 0.0)
        table = jnp.where(position < live_ref[:, step_at : step_at + 1], table, 0.0)
        high = table.astype(BF16).astype(F32)
        rest = table - high
        middle = rest.astype(BF16).astype(F32)
        low = rest - middle
        split = jnp.where(third == 0, high, jnp.where(third == 1, middle, low))
        split = jnp.where(lane < 3 * expert_count, split, 0.0)
        out_ref[rows, pl.ds(width, LANES)] = split.astype(BF16)
    for share_ref in shares:
        features = share_ref.shape[2]
        for at in range(share_ref.shape[0]):
            share_ref[at] = out_ref[:, pl.ds(at * features, features)]


def make_payload(tokens, live_rows, expert_ids, gate_weights, norm_gain, expert_count, share_count):
    step_count, row_count, width = tokens.shape
    height, features = step_count * row_count, width // share_count
    inputs = (live_rows, tokens, expert_ids, gate_weights, norm_gain)
    aligned = features % LANES == 0
    shapes = [jax.ShapeDtypeStruct((height, width + LANES), BF16)]
    if aligned:
        shapes.append(jax.ShapeDtypeStruct((share_count, height, features), BF16))
    results = pl.pallas_call(
        functools.partial(payload_kernel, expert_count),
        out_shape=shapes,
        in_specs=[hbm_spec()] * 5,
        out_specs=[vmem_spec()] * len(shapes),
        scratch_shapes=[pltpu.VMEM(value.shape, value.dtype) for value in inputs] + [pltpu.SemaphoreType.DMA((5,))],
        compiler_params=small_grant(),
        cost_estimate=pl.CostEstimate(flops=8 * tokens.size, bytes_accessed=6 * tokens.size, transcendentals=0),
    )(*[in_hbm(value) for value in inputs])
    if aligned:
        return results
    payload = results[0]
    return payload, jnp.swapaxes(payload[:, :width].reshape(height, share_count, features), 0, 1)


def join_kernel(heights, keep_ref, come_ref, *outs):
    at = 0
    for height, out_ref in zip(heights, outs, strict=True):
        rows = pl.ds(at, height)
        out_ref[...] = (keep_ref[rows, :].astype(F32) + come_ref[rows, :].astype(F32)).astype(out_ref.dtype)
        at += height


def join(keep, come, heights):
    columns = keep.shape[1]
    return pl.pallas_call(
        functools.partial(join_kernel, heights),
        out_shape=[
            jax.ShapeDtypeStruct((height, columns), F32 if at == 0 else BF16) for at, height in enumerate(heights)
        ],
        in_specs=[vmem_spec()] * 2,
        out_specs=[vmem_spec()] * len(heights),
        compiler_params=small_grant(),
        cost_estimate=pl.CostEstimate(flops=keep.size, bytes_accessed=8 * keep.size, transcendentals=0),
    )(keep, come)


def pair_copies(own_hbm, other_hbm, weight_ref, sems):
    features = own_hbm.shape[0]
    core = lax.rem(lax.axis_index("expert"), 2)
    own_at = pl.multiple_of(core * features, 16)
    other_at = pl.multiple_of((1 - core) * features, 16)
    own = pltpu.make_async_copy(own_hbm, weight_ref.at[pl.ds(own_at, features), :], sems.at[0])
    other = pltpu.make_async_copy(other_hbm, weight_ref.at[pl.ds(other_at, features), :], sems.at[1])
    return own, other


def shared_up_kernel(blocks_ref, own_hbm, other_hbm, out_ref, rows_ref, weight_ref, sems):
    count, height, _ = blocks_ref.shape
    own, other = pair_copies(own_hbm, other_hbm, weight_ref, sems)
    own.start()
    other.start()
    for at in range(count):
        rows_ref[pl.ds(at * height, height), :] = blocks_ref[at]
    own.wait()
    other.wait()
    partial_value = jnp.dot(rows_ref[...], weight_ref[...], preferred_element_type=F32).astype(BF16)
    for at in range(count):
        out_ref[at] = partial_value[at * height : (at + 1) * height]


def shared_down_kernel(blocks_ref, own_hbm, other_hbm, out_ref, rows_ref, weight_ref, sems):
    count, height, _ = blocks_ref.shape
    own, other = pair_copies(own_hbm, other_hbm, weight_ref, sems)
    own.start()
    other.start()
    for at in range(count):
        rows_ref[pl.ds(at * height, height), :] = blocks_ref[at]
    own.wait()
    other.wait()
    contract = (((1,), (1,)), ((), ()))
    result = lax.dot_general(rows_ref[...], weight_ref[...], contract, preferred_element_type=F32).astype(BF16)
    for at in range(count):
        out_ref[at] = result[at * height : (at + 1) * height]


def shared_matmul(kernel, blocks, own, other, columns):
    count, height, depth = blocks.shape
    return pl.pallas_call(
        kernel,
        out_shape=jax.ShapeDtypeStruct((count, height, columns), BF16),
        in_specs=[vmem_spec()] + [hbm_spec()] * 2,
        out_specs=vmem_spec(),
        scratch_shapes=[
            pltpu.VMEM((count * height, depth), BF16),
            pltpu.VMEM((2 * own.shape[0], own.shape[1]), BF16),
            pltpu.SemaphoreType.DMA((2,)),
        ],
        compiler_params=small_grant(),
        cost_estimate=pl.CostEstimate(
            flops=2 * count * height * depth * columns, bytes_accessed=2 * depth * columns, transcendentals=0
        ),
    )(blocks, in_hbm(own), in_hbm(other))


def shared_hidden_kernel(parts_ref, out_ref):
    count, _, columns = parts_ref.shape
    total = parts_ref[0].astype(F32)
    for at in range(1, count):
        total = total + parts_ref[at].astype(F32)
    half = columns // 2
    hidden = (jax.nn.silu(total[:, :half]) * total[:, half:]).astype(BF16)
    for at in range(count):
        out_ref[at] = hidden


def shared_hidden(parts):
    count, height, columns = parts.shape
    return pl.pallas_call(
        shared_hidden_kernel,
        out_shape=jax.ShapeDtypeStruct((count, height, columns // 2), BF16),
        in_specs=[vmem_spec()],
        out_specs=vmem_spec(),
        compiler_params=small_grant(),
        cost_estimate=pl.CostEstimate(flops=parts.size, bytes_accessed=3 * parts.size, transcendentals=height * columns),
    )(parts)


def routed_up_kernel(block_count, expert_count, step, *refs):
    blocks = refs[:block_count]
    weight_hbm, hidden_ref, gate_ref, rows_ref, total_ref, near_ref, sems = refs[block_count:]
    height = blocks[0].shape[0]
    width, double = weight_hbm.shape
    units = double // 2
    count, slots = width // step, near_ref.shape[0]

    def fetch(at):
        slot = lax.rem(at, slots)
        rows = pl.ds(pl.multiple_of(at * step, step), step)
        return pltpu.make_async_copy(weight_hbm.at[rows, :], near_ref.at[slot], sems.at[slot])

    for at in range(min(slots, count)):
        fetch(jnp.int32(at)).start()

    expert = lax.div(lax.axis_index("expert"), lax.axis_size("expert") // expert_count)
    lane = lax.broadcasted_iota(jnp.int32, (height, LANES), 1)
    mine = (lane == expert) | (lane == expert + expert_count) | (lane == expert + 2 * expert_count)
    for at, block in enumerate(blocks):
        rows = pl.ds(at * height, height)
        rows_ref[rows, :] = block[:, pl.ds(0, width)]
        table = jnp.where(mine, block[:, pl.ds(width, LANES)].astype(F32), 0.0)
        gate_ref[rows, :] = jnp.broadcast_to(jnp.sum(table, axis=1, keepdims=True), (height, LANES))
    total_ref[...] = jnp.zeros_like(total_ref)

    def body(at, carry):
        fetch(at).wait()
        columns = pl.ds(pl.multiple_of(at * step, LANES), step)
        total_ref[...] += jnp.dot(rows_ref[:, columns], near_ref[lax.rem(at, slots)], preferred_element_type=F32)

        @pl.when(at + slots < count)
        def _():
            fetch(at + slots).start()

        return carry

    lax.fori_loop(0, count, body, 0)
    hidden_ref[...] = (jax.nn.silu(total_ref[:, :units]) * total_ref[:, units:]).astype(BF16)


def routed_up(blocks, weight, expert_count):
    height = blocks[0].shape[0]
    width, double = weight.shape
    rows = len(blocks) * height
    step = largest_step(width, 2 * LANES, UP_STEP)
    return pl.pallas_call(
        functools.partial(routed_up_kernel, len(blocks), expert_count, step),
        out_shape=[jax.ShapeDtypeStruct((rows, double // 2), BF16), jax.ShapeDtypeStruct((rows, LANES), F32)],
        in_specs=[vmem_spec()] * len(blocks) + [hbm_spec()],
        out_specs=[vmem_spec()] * 2,
        scratch_shapes=[
            pltpu.VMEM((rows, width), BF16),
            pltpu.VMEM((rows, double), F32),
            pltpu.VMEM((UP_SLOTS, step, double), BF16),
            pltpu.SemaphoreType.DMA((UP_SLOTS,)),
        ],
        compiler_params=pltpu.CompilerParams(vmem_limit_bytes=ROUTED_GRANT),
        cost_estimate=pl.CostEstimate(
            flops=2 * rows * width * double, bytes_accessed=2 * width * double, transcendentals=rows * double // 2
        ),
    )(*blocks, in_hbm(weight))


def routed_down_kernel(step, hidden_ref, gate_ref, weight_hbm, *refs):
    outs = refs[: 2 * COLUMN_PARTS]
    near_ref, sems = refs[2 * COLUMN_PARTS :]
    half_rows = hidden_ref.shape[0] // 2
    count, slots = weight_hbm.shape[1] // step, near_ref.shape[0]

    def fetch(at):
        slot = lax.rem(at, slots)
        columns = pl.ds(pl.multiple_of(at * step, LANES), step)
        return pltpu.make_async_copy(weight_hbm.at[:, columns], near_ref.at[slot], sems.at[slot])

    for at in range(min(slots, count)):
        fetch(jnp.int32(at)).start()
    gate = gate_ref[:, :1]
    per_part = count // COLUMN_PARTS
    for part in range(COLUMN_PARTS):
        keep_ref, send_ref = outs[2 * part], outs[2 * part + 1]

        def body(at, carry, part=part, keep_ref=keep_ref, send_ref=send_ref):
            whole_at = part * per_part + at
            fetch(whole_at).wait()
            result = jnp.dot(hidden_ref[...], near_ref[lax.rem(whole_at, slots)], preferred_element_type=F32)
            weighted = (result.astype(BF16).astype(F32) * gate).astype(BF16)
            columns = pl.ds(pl.multiple_of(at * step, LANES), step)
            keep_ref[:, columns] = weighted[:half_rows]
            send_ref[:, columns] = weighted[half_rows:]

            @pl.when(whole_at + slots < count)
            def _():
                fetch(whole_at + slots).start()

            return carry

        lax.fori_loop(0, per_part, body, 0)


def routed_down(hidden, gate, weight):
    rows, units = hidden.shape
    width = weight.shape[1]
    part_width = width // COLUMN_PARTS
    step = largest_step(part_width, LANES, DOWN_STEP)
    shape = jax.ShapeDtypeStruct((rows // 2, part_width), BF16)
    return pl.pallas_call(
        functools.partial(routed_down_kernel, step),
        out_shape=[shape] * (2 * COLUMN_PARTS),
        in_specs=[vmem_spec()] * 2 + [hbm_spec()],
        out_specs=[vmem_spec()] * (2 * COLUMN_PARTS),
        scratch_shapes=[pltpu.VMEM((DOWN_SLOTS, units, step), BF16), pltpu.SemaphoreType.DMA((DOWN_SLOTS,))],
        compiler_params=pltpu.CompilerParams(vmem_limit_bytes=ROUTED_GRANT),
        cost_estimate=pl.CostEstimate(
            flops=2 * rows * width * units, bytes_accessed=2 * width * units, transcendentals=0
        ),
    )(hidden, gate, in_hbm(weight))


def finish_kernel(part_count, near_count, live_ref, tokens_ref, shared_ref, *refs):
    out_ref, total_ref = refs[-2], refs[-1]
    lines = refs[:-2]
    step_count, row_count, width = tokens_ref.shape
    part_width = width // part_count
    for part in range(part_count):
        total = lines[part * near_count][...]
        for at in range(1, near_count):
            total = total + lines[part * near_count + at][...].astype(F32)
        total_ref[:, pl.ds(part * part_width, part_width)] = total
    features = shared_ref.shape[2]
    for at in range(shared_ref.shape[0]):
        total_ref[:, pl.ds(at * features, features)] += shared_ref[at].astype(F32)
    position = lax.broadcasted_iota(jnp.int32, (row_count, width), 0)
    for step_at in range(step_count):
        added = total_ref[pl.ds(step_at * row_count, row_count), :]
        masked = jnp.where(position < live_ref[:, step_at : step_at + 1], added, 0.0)
        out_ref[step_at] = (tokens_ref[step_at].astype(F32) + masked).astype(BF16)


def finish(tokens, live_rows, shared, lines):
    step_count, row_count, width = tokens.shape
    height = step_count * row_count
    if shared.shape[2] % LANES != 0:
        shared = jnp.swapaxes(shared, 0, 1).reshape(1, height, width)
    near_count = len(lines[0])
    flat = [line for group in lines for line in group]
    return pl.pallas_call(
        functools.partial(finish_kernel, len(lines), near_count),
        out_shape=jax.ShapeDtypeStruct(tokens.shape, BF16),
        in_specs=[vmem_spec()] * (3 + len(flat)),
        out_specs=vmem_spec(),
        scratch_shapes=[pltpu.VMEM((height, width), F32)],
        compiler_params=small_grant(),
        cost_estimate=pl.CostEstimate(flops=8 * tokens.size, bytes_accessed=12 * tokens.size, transcendentals=0),
    )(live_rows, tokens, shared, *flat)


def per_device(
    tokens,
    live_rows,
    expert_ids,
    gate_weights,
    norm_gain,
    expert_gate_up,
    expert_down,
    shared_gate_up,
    shared_down,
):
    device_count = lax.axis_size("expert")
    line_count = device_count // 4
    height = tokens.shape[0] * tokens.shape[1]
    live = jnp.swapaxes(live_rows, 0, 1)

    def swap(value, mask):
        return lax.ppermute(value, "expert", [(i, i ^ mask) for i in range(device_count)])

    def swap_line(values):
        return [swap(value, 4 * k) for k, value in enumerate(values, 1)]

    groups = [[first + 2 * at for at in range(device_count // 2)] for first in range(2)]

    def exchange(value):
        return lax.all_to_all(value, "expert", 0, 0, axis_index_groups=groups, tiled=True)

    own_up, own_down = shared_gate_up[0], jnp.swapaxes(shared_down[0], 0, 1)
    other_up, other_down = swap(own_up, 1), swap(own_down, 1)
    payload, shares = make_payload(
        tokens, live, expert_ids, gate_weights, norm_gain, EXPERTS, device_count // 2
    )

    along = [payload] + swap_line([payload] * (line_count - 1))
    across = [swap(block, 2) for block in along]
    same = along + across
    beside = [swap(block, 1) for block in same]

    partial_value = shared_matmul(shared_up_kernel, exchange(shares), own_up, other_up, own_up.shape[1])
    up_weight, down_weight = expert_gate_up[0, 0], expert_down[0, 0]
    up_weight, partial_value = lax.optimization_barrier((up_weight, partial_value))
    routed_hidden, gate = routed_up(same + beside, up_weight, EXPERTS)
    hidden = shared_hidden(exchange(partial_value))
    down_weight, hidden = lax.optimization_barrier((down_weight, hidden))
    outs = routed_down(routed_hidden, gate, down_weight)
    shared = exchange(
        shared_matmul(shared_down_kernel, exchange(hidden), own_down, other_down, 2 * own_down.shape[0])
    )
    lines = []
    for part in range(COLUMN_PARTS):
        keep, send = outs[2 * part], outs[2 * part + 1]
        keep, send = join(keep, swap(send, 1), [line_count * height] * 2)
        near = list(join(keep, swap(send, 2), [height] * line_count))
        lines.append(near[:1] + swap_line(near[1:]))
    return finish(tokens, live, shared, lines)


def solution(mesh):
    placed = (
        P(None, ("parts", "expert"), None),
        P(None, ("parts", "expert")),
        P(None, None, ("parts", "expert"), None),
        P(None, None, ("parts", "expert"), None),
        P(),
        P(None, "expert", None, None),
        P(None, "expert", None, None),
        P(None, "expert", None),
        P(None, None, "expert"),
    )
    return jax.shard_map(
        per_device,
        mesh=mesh,
        in_specs=placed,
        out_specs=P(None, ("parts", "expert"), None),
        check_vma=False,
    )
```

```python
import functools
import math

import jax
import jax.numpy as jnp
from jax import lax
from jax.experimental import pallas as pl
from jax.experimental.pallas import tpu as pltpu
from jax.sharding import PartitionSpec as P


EXPERTS = 16
EPSILON = 1e-06
LANES = 128
SMALL_GRANT = 8 << 20
FIRST_EIGHTHS = 5
ROUTED_GRANT = 40 << 20
UP_STEP, UP_SLOTS = 512, 6
DOWN_STEP, DOWN_SLOTS = 896, 8


F32 = jnp.float32
BF16 = jnp.bfloat16


def vmem_spec():
    return pl.BlockSpec(memory_space=pltpu.VMEM)


def any_spec():
    return pl.BlockSpec(memory_space=pl.ANY)


def hbm_spec():
    return pl.BlockSpec(memory_space=pltpu.HBM)


def in_hbm(value):
    return pltpu.with_memory_space_constraint(value, pltpu.HBM)


def small_grant():
    return pltpu.CompilerParams(vmem_limit_bytes=SMALL_GRANT)


def largest_step(total, unit, limit):
    best = None
    for step in range(unit, limit + 1, unit):
        if total % step == 0:
            best = step
    return best if best is not None else total


def payload_kernel(expert_count, *refs):
    inputs, rest = refs[:5], refs[5:]
    out_ref, near, sems = rest[0], rest[1:6], rest[6]
    copies = [pltpu.make_async_copy(inputs[at], near[at], sems.at[at]) for at in range(5)]
    for copy in copies:
        copy.start()
    for copy in copies:
        copy.wait()
    live_ref, tokens_ref, ids_ref, gates_ref, gain_ref = near
    step_count, row_count, width = tokens_ref.shape
    top_count = ids_ref.shape[3]
    lane = lax.broadcasted_iota(jnp.int32, (row_count, LANES), 1)
    position = lax.broadcasted_iota(jnp.int32, (row_count, LANES), 0)
    third = jnp.where(lane >= 2 * expert_count, 2, jnp.where(lane >= expert_count, 1, 0))
    named = lane - third * expert_count
    for step_at in range(step_count):
        rows = pl.ds(step_at * row_count, row_count)
        widened = tokens_ref[step_at].astype(F32)
        scaling = lax.rsqrt(jnp.sum(widened * widened, axis=-1, keepdims=True) / width + EPSILON)
        out_ref[rows, pl.ds(0, width)] = (widened * scaling * gain_ref[...]).astype(BF16)
        table = jnp.zeros((row_count, LANES), F32)
        for k in range(top_count):
            chosen = ids_ref[0, step_at, :, k : k + 1]
            gate = gates_ref[0, step_at, :, k : k + 1]
            table = table + jnp.where(named == chosen, gate, 0.0)
        table = jnp.where(position < live_ref[:, step_at : step_at + 1], table, 0.0)
        high = table.astype(BF16).astype(F32)
        rest = table - high
        middle = rest.astype(BF16).astype(F32)
        low = rest - middle
        split = jnp.where(third == 0, high, jnp.where(third == 1, middle, low))
        split = jnp.where(lane < 3 * expert_count, split, 0.0)
        out_ref[rows, pl.ds(width, LANES)] = split.astype(BF16)


def make_payload(tokens, live_rows, expert_ids, gate_weights, norm_gain, expert_count):
    step_count, row_count, width = tokens.shape
    inputs = (live_rows, tokens, expert_ids, gate_weights, norm_gain)
    return pl.pallas_call(
        functools.partial(payload_kernel, expert_count),
        out_shape=jax.ShapeDtypeStruct((step_count * row_count, width + LANES), BF16),
        in_specs=[hbm_spec()] * 5,
        out_specs=vmem_spec(),
        scratch_shapes=[pltpu.VMEM(value.shape, value.dtype) for value in inputs] + [pltpu.SemaphoreType.DMA((5,))],
        compiler_params=small_grant(),
        cost_estimate=pl.CostEstimate(flops=8 * tokens.size, bytes_accessed=6 * tokens.size, transcendentals=0),
    )(*[in_hbm(value) for value in inputs])


def join_kernel(count, height, picks, masks, first_column, *refs):
    operands, outs = refs[:count], refs[len(refs) - len(picks) :]

    def total(block, columns):
        rows = pl.ds(block * height, height)
        value = operands[0][rows, columns].astype(F32)
        for operand in operands[1:]:
            value = value + operand[rows, columns].astype(F32)
        return value

    for blocks, out_ref in zip(picks, outs, strict=True):
        for at, block in enumerate(blocks):
            out_ref[pl.ds(at * height, height), :] = total(block, slice(None)).astype(out_ref.dtype)
    if not masks:
        return
    shared_ref = refs[count]
    features, width = shared_ref.shape[2], operands[0].shape[1]
    group = lax.div(lax.axis_index("expert"), 2)
    start = group * features - first_column

    @pl.when((start >= 0) & (start < width))
    def _():
        columns = pl.ds(pl.multiple_of(start, LANES), features)
        for blocks, out_ref in zip(picks, outs, strict=True):
            for at, block in enumerate(blocks):
                value = total(block, columns) + shared_ref[jnp.bitwise_xor(group, masks[block])].astype(F32)
                out_ref[pl.ds(at * height, height), columns] = value.astype(out_ref.dtype)


def join(operands, height, picks, shared=None, masks=(), first_column=0):
    columns = operands[0].shape[1]
    size = operands[0].size
    extra = [] if shared is None else [shared]
    return list(
        pl.pallas_call(
            functools.partial(
                join_kernel, len(operands), height, picks, () if shared is None else masks, first_column
            ),
            out_shape=[
                jax.ShapeDtypeStruct((len(blocks) * height, columns), F32 if at == 0 else BF16)
                for at, blocks in enumerate(picks)
            ],
            in_specs=[vmem_spec()] * (len(operands) + len(extra)),
            out_specs=[vmem_spec()] * len(picks),
            compiler_params=small_grant(),
            cost_estimate=pl.CostEstimate(
                flops=len(operands) * size, bytes_accessed=(2 * len(operands) + 4) * size, transcendentals=0
            ),
        )(*operands, *extra)
    )


def pair_copies(own_hbm, other_hbm, weight_ref, sems):
    features = own_hbm.shape[0]
    core = lax.rem(lax.axis_index("expert"), 2)
    own_at = pl.multiple_of(core * features, 16)
    other_at = pl.multiple_of((1 - core) * features, 16)
    own = pltpu.make_async_copy(own_hbm, weight_ref.at[pl.ds(own_at, features), :], sems.at[0])
    other = pltpu.make_async_copy(other_hbm, weight_ref.at[pl.ds(other_at, features), :], sems.at[1])
    return own, other


def shared_up_kernel(masks, *refs):
    blocks = refs[: len(masks)]
    own_hbm, other_hbm, out_ref, rows_ref, weight_ref, sems = refs[len(masks) :]
    height, width = blocks[0].shape
    features = weight_ref.shape[0]
    own, other = pair_copies(own_hbm, other_hbm, weight_ref, sems)
    own.start()
    other.start()
    group = lax.div(lax.axis_index("expert"), 2)
    start = 0 if width == features else pl.multiple_of(group * features, LANES)
    for at, block in enumerate(blocks):
        rows_ref[pl.ds(at * height, height), :] = block[:, pl.ds(start, features)]
    own.wait()
    other.wait()
    partial_value = jnp.dot(rows_ref[...], weight_ref[...], preferred_element_type=F32).astype(BF16)
    for at, mask in enumerate(masks):
        out_ref[jnp.bitwise_xor(group, mask)] = partial_value[at * height : (at + 1) * height]


def shared_up(blocks, masks, own, other):
    count, height = len(blocks), blocks[0].shape[0]
    features, columns = 2 * own.shape[0], own.shape[1]
    if features % LANES != 0:
        first = lax.axis_index("expert") // 2 * features
        blocks = [lax.dynamic_slice_in_dim(block, first, features, 1) for block in blocks]
    return pl.pallas_call(
        functools.partial(shared_up_kernel, masks),
        out_shape=jax.ShapeDtypeStruct((count, height, columns), BF16),
        in_specs=[vmem_spec()] * count + [any_spec()] * 2,
        out_specs=vmem_spec(),
        scratch_shapes=[
            pltpu.VMEM((count * height, features), BF16),
            pltpu.VMEM((features, columns), BF16),
            pltpu.SemaphoreType.DMA((2,)),
        ],
        compiler_params=small_grant(),
        cost_estimate=pl.CostEstimate(
            flops=2 * count * height * features * columns, bytes_accessed=2 * features * columns, transcendentals=0
        ),
    )(*blocks, in_hbm(own), other)


def shared_down_kernel(blocks_ref, own_hbm, other_hbm, out_ref, rows_ref, weight_ref, sems):
    count, height, _ = blocks_ref.shape
    own, other = pair_copies(own_hbm, other_hbm, weight_ref, sems)
    own.start()
    other.start()
    for at in range(count):
        rows_ref[pl.ds(at * height, height), :] = blocks_ref[at]
    own.wait()
    other.wait()
    contract = (((1,), (1,)), ((), ()))
    result = lax.dot_general(rows_ref[...], weight_ref[...], contract, preferred_element_type=F32).astype(BF16)
    for at in range(count):
        out_ref[at] = result[at * height : (at + 1) * height]


def shared_down_rows(blocks, own, other):
    count, height, depth = blocks.shape
    features = 2 * own.shape[0]
    return pl.pallas_call(
        shared_down_kernel,
        out_shape=jax.ShapeDtypeStruct((count, height, features), BF16),
        in_specs=[vmem_spec()] + [any_spec()] * 2,
        out_specs=vmem_spec(),
        scratch_shapes=[
            pltpu.VMEM((count * height, depth), BF16),
            pltpu.VMEM((features, depth), BF16),
            pltpu.SemaphoreType.DMA((2,)),
        ],
        compiler_params=small_grant(),
        cost_estimate=pl.CostEstimate(
            flops=2 * count * height * depth * features, bytes_accessed=2 * depth * features, transcendentals=0
        ),
    )(blocks, in_hbm(own), other)


def shared_hidden_kernel(parts_ref, out_ref):
    count, _, columns = parts_ref.shape
    total = parts_ref[0].astype(F32)
    for at in range(1, count):
        total = total + parts_ref[at].astype(F32)
    half = columns // 2
    hidden = (jax.nn.silu(total[:, :half]) * total[:, half:]).astype(BF16)
    for at in range(count):
        out_ref[at] = hidden


def shared_hidden(parts):
    count, height, columns = parts.shape
    return pl.pallas_call(
        shared_hidden_kernel,
        out_shape=jax.ShapeDtypeStruct((count, height, columns // 2), BF16),
        in_specs=[vmem_spec()],
        out_specs=vmem_spec(),
        compiler_params=small_grant(),
        cost_estimate=pl.CostEstimate(flops=parts.size, bytes_accessed=3 * parts.size, transcendentals=height * columns),
    )(parts)


def routed_up_kernel(block_count, expert_count, step, *refs):
    blocks = refs[:block_count]
    weight_hbm, hidden_ref, gate_ref, rows_ref, total_ref, near_ref, sems = refs[block_count:]
    height = blocks[0].shape[0]
    width, double = weight_hbm.shape
    units = double // 2
    count, slots = width // step, near_ref.shape[0]

    def fetch(at):
        slot = lax.rem(at, slots)
        rows = pl.ds(pl.multiple_of(at * step, step), step)
        return pltpu.make_async_copy(weight_hbm.at[rows, :], near_ref.at[slot], sems.at[slot])

    for at in range(min(slots, count)):
        fetch(jnp.int32(at)).start()

    expert = lax.div(lax.axis_index("expert"), lax.axis_size("expert") // expert_count)
    lane = lax.broadcasted_iota(jnp.int32, (height, LANES), 1)
    mine = (lane == expert) | (lane == expert + expert_count) | (lane == expert + 2 * expert_count)
    for at, block in enumerate(blocks):
        rows = pl.ds(at * height, height)
        rows_ref[rows, :] = block[:, pl.ds(0, width)]
        table = jnp.where(mine, block[:, pl.ds(width, LANES)].astype(F32), 0.0)
        gate_ref[rows, :] = jnp.broadcast_to(jnp.sum(table, axis=1, keepdims=True), (height, LANES))
    total_ref[...] = jnp.zeros_like(total_ref)

    def body(at, carry):
        fetch(at).wait()
        columns = pl.ds(pl.multiple_of(at * step, LANES), step)
        total_ref[...] += jnp.dot(rows_ref[:, columns], near_ref[lax.rem(at, slots)], preferred_element_type=F32)

        @pl.when(at + slots < count)
        def _():
            fetch(at + slots).start()

        return carry

    lax.fori_loop(0, count, body, 0)
    hidden_ref[...] = (jax.nn.silu(total_ref[:, :units]) * total_ref[:, units:]).astype(BF16)


def routed_up(blocks, weight, expert_count):
    height = blocks[0].shape[0]
    width, double = weight.shape
    rows = len(blocks) * height
    step = largest_step(width, 2 * LANES, UP_STEP)
    return pl.pallas_call(
        functools.partial(routed_up_kernel, len(blocks), expert_count, step),
        out_shape=[jax.ShapeDtypeStruct((rows, double // 2), BF16), jax.ShapeDtypeStruct((rows, LANES), F32)],
        in_specs=[vmem_spec()] * len(blocks) + [hbm_spec()],
        out_specs=[vmem_spec()] * 2,
        scratch_shapes=[
            pltpu.VMEM((rows, width), BF16),
            pltpu.VMEM((rows, double), F32),
            pltpu.VMEM((UP_SLOTS, step, double), BF16),
            pltpu.SemaphoreType.DMA((UP_SLOTS,)),
        ],
        compiler_params=pltpu.CompilerParams(vmem_limit_bytes=ROUTED_GRANT),
        cost_estimate=pl.CostEstimate(
            flops=2 * rows * width * double, bytes_accessed=2 * width * double, transcendentals=rows * double // 2
        ),
    )(*blocks, in_hbm(weight))


def routed_down_kernel(step, part_count, hidden_ref, gate_ref, weight_hbm, *refs):
    outs = refs[: 2 * part_count]
    near_ref, sems = refs[2 * part_count :]
    half_rows = hidden_ref.shape[0] // 2
    count, slots = weight_hbm.shape[1] // step, near_ref.shape[0]

    def fetch(at):
        slot = lax.rem(at, slots)
        columns = pl.ds(pl.multiple_of(at * step, LANES), step)
        return pltpu.make_async_copy(weight_hbm.at[:, columns], near_ref.at[slot], sems.at[slot])

    for at in range(min(slots, count)):
        fetch(jnp.int32(at)).start()
    gate = gate_ref[:, :1]
    first = 0
    for part in range(part_count):
        keep_ref, send_ref = outs[2 * part], outs[2 * part + 1]
        in_part = keep_ref.shape[1] // step

        def body(at, carry, first=first, keep_ref=keep_ref, send_ref=send_ref):
            whole_at = first + at
            fetch(whole_at).wait()
            result = jnp.dot(hidden_ref[...], near_ref[lax.rem(whole_at, slots)], preferred_element_type=F32)
            weighted = (result.astype(BF16).astype(F32) * gate).astype(BF16)
            columns = pl.ds(pl.multiple_of(at * step, LANES), step)
            keep_ref[:, columns] = weighted[:half_rows]
            send_ref[:, columns] = weighted[half_rows:]

            @pl.when(whole_at + slots < count)
            def _():
                fetch(whole_at + slots).start()

            return carry

        lax.fori_loop(0, in_part, body, 0)
        first += in_part


def routed_down(hidden, gate, weight, widths):
    rows, units = hidden.shape
    width = weight.shape[1]
    step = largest_step(math.gcd(*widths), LANES, DOWN_STEP)
    return pl.pallas_call(
        functools.partial(routed_down_kernel, step, len(widths)),
        out_shape=[jax.ShapeDtypeStruct((rows // 2, columns), BF16) for columns in widths for _ in range(2)],
        in_specs=[vmem_spec()] * 2 + [hbm_spec()],
        out_specs=[vmem_spec()] * (2 * len(widths)),
        scratch_shapes=[pltpu.VMEM((DOWN_SLOTS, units, step), BF16), pltpu.SemaphoreType.DMA((DOWN_SLOTS,))],
        compiler_params=pltpu.CompilerParams(vmem_limit_bytes=ROUTED_GRANT),
        cost_estimate=pl.CostEstimate(
            flops=2 * rows * width * units, bytes_accessed=2 * width * units, transcendentals=0
        ),
    )(hidden, gate, in_hbm(weight))


def finish_kernel(counts, live_ref, tokens_ref, *refs):
    out_ref = refs[-1]
    step_count, row_count, _ = tokens_ref.shape
    used, first = 0, 0
    for count in counts:
        total = refs[used][...]
        for at in range(1, count):
            total = total + refs[used + at][...].astype(F32)
        width = total.shape[1]
        position = lax.broadcasted_iota(jnp.int32, (row_count, width), 0)
        columns = pl.ds(first, width)
        for step_at in range(step_count):
            added = total[step_at * row_count : (step_at + 1) * row_count]
            masked = jnp.where(position < live_ref[:, step_at : step_at + 1], added, 0.0)
            out_ref[step_at, :, columns] = (tokens_ref[step_at, :, columns].astype(F32) + masked).astype(BF16)
        used += count
        first += width


def finish(tokens, live_rows, lines):
    flat = [line for group in lines for line in group]
    return pl.pallas_call(
        functools.partial(finish_kernel, [len(group) for group in lines]),
        out_shape=jax.ShapeDtypeStruct(tokens.shape, BF16),
        in_specs=[vmem_spec()] * (2 + len(flat)),
        out_specs=vmem_spec(),
        compiler_params=small_grant(),
        cost_estimate=pl.CostEstimate(flops=8 * tokens.size, bytes_accessed=12 * tokens.size, transcendentals=0),
    )(live_rows, tokens, *flat)


def per_device(
    tokens,
    live_rows,
    expert_ids,
    gate_weights,
    norm_gain,
    expert_gate_up,
    expert_down,
    shared_gate_up,
    shared_down,
):
    device_count = lax.axis_size("expert")
    line_count = device_count // 4
    height = tokens.shape[0] * tokens.shape[1]
    live = jnp.swapaxes(live_rows, 0, 1)

    def swap(value, mask):
        return lax.ppermute(value, "expert", [(i, i ^ mask) for i in range(device_count)])

    def swap_line(values):
        swapped = []
        for k, value in enumerate(values, 1):
            swapped.append(swap(value, 4 * k))
        return swapped

    groups = [[first + 2 * at for at in range(device_count // 2)] for first in range(2)]

    def exchange(value):
        return lax.all_to_all(value, "expert", 0, 0, axis_index_groups=groups, tiled=True)

    own_up, own_down = shared_gate_up[0], jnp.swapaxes(shared_down[0], 0, 1)
    other_up, other_down = swap(own_up, 1), swap(own_down, 1)
    payload = make_payload(tokens, live, expert_ids, gate_weights, norm_gain, EXPERTS)
    along = [payload] + swap_line([payload] * (line_count - 1))
    across = []
    for block in along:
        across.append(swap(block, 2))
    same = along + across
    masks = [2 * k for k in range(line_count)] + [2 * k + 1 for k in range(line_count)]
    beside = [swap(block, 1) for block in same]

    partial_value = shared_up(same, masks, own_up, other_up)
    width, features = tokens.shape[2], 2 * own_down.shape[0]
    unit = features if features % LANES == 0 else LANES
    first_width = (width // unit * FIRST_EIGHTHS + 4) // 8 * unit
    widths = [first_width, width - first_width]
    up_weight, down_weight = expert_gate_up[0, 0], expert_down[0, 0]
    up_weight, partial_value = lax.optimization_barrier((up_weight, partial_value))
    projected = exchange(partial_value)
    routed_hidden, gate = routed_up(same + beside, up_weight, EXPERTS)
    hidden = shared_hidden(projected)
    down_weight, hidden = lax.optimization_barrier((down_weight, hidden))
    spread = exchange(hidden)
    outs = routed_down(routed_hidden, gate, down_weight, widths)
    shared = shared_down_rows(spread, own_down, other_down)

    come = []
    for part in range(2):
        come.append(swap(outs[2 * part + 1], 1))
    lower, upper = list(range(line_count)), list(range(line_count, 2 * line_count))
    picks = ([lower, upper], [[k, line_count + k] for k in range(line_count)])
    joined = []
    for part in range(2):
        first = part * widths[0]
        if features % LANES == 0:
            joined.append(join([outs[2 * part], come[part]], height, picks[part], shared, masks, first))
        else:
            group = lax.axis_index("expert") // 2
            rows = shared[jnp.bitwise_xor(jnp.asarray(masks), group)].reshape(-1, features)
            wide = lax.dynamic_update_slice(
                jnp.zeros((rows.shape[0], width), BF16), rows, (0, group * features)
            )
            piece = wide[:, first : first + widths[part]]
            joined.append(join([outs[2 * part], come[part], piece], height, picks[part]))
    come_across = swap(joined[0][1], 2)
    come_along = swap_line(joined[1][1:])
    near = join([joined[0][0], come_across], height, [[k] for k in range(line_count)])
    first_lines = near[:1] + swap_line(near[1:])
    keep, send = join([joined[1][0]] + come_along, height, [[0], [1]])
    second_lines = [keep, swap(send, 2)]
    return finish(tokens, live, [first_lines, second_lines])


def solution(mesh):
    placed = (
        P(None, ("parts", "expert"), None),
        P(None, ("parts", "expert")),
        P(None, None, ("parts", "expert"), None),
        P(None, None, ("parts", "expert"), None),
        P(),
        P(None, "expert", None, None),
        P(None, "expert", None, None),
        P(None, "expert", None),
        P(None, None, "expert"),
    )
    return jax.shard_map(
        per_device,
        mesh=mesh,
        in_specs=placed,
        out_specs=P(None, ("parts", "expert"), None),
        check_vma=False,
    )
```

```python
import functools
import math

import jax
import jax.numpy as jnp
from jax import lax
from jax.experimental import pallas as pl
from jax.experimental.pallas import tpu as pltpu
from jax.sharding import PartitionSpec as P


EXPERTS = 16
EPSILON = 1e-06
LANES = 128
SMALL_GRANT = 8 << 20
FIRST_EIGHTHS = 5
ROUTED_GRANT = 40 << 20
UP_STEP, UP_SLOTS = 512, 6
DOWN_STEP, DOWN_SLOTS = 896, 8


F32 = jnp.float32
BF16 = jnp.bfloat16


def vmem_spec():
    return pl.BlockSpec(memory_space=pltpu.VMEM)


def any_spec():
    return pl.BlockSpec(memory_space=pl.ANY)


def hbm_spec():
    return pl.BlockSpec(memory_space=pltpu.HBM)


def in_hbm(value):
    return pltpu.with_memory_space_constraint(value, pltpu.HBM)


def small_grant():
    return pltpu.CompilerParams(vmem_limit_bytes=SMALL_GRANT)


def largest_step(total, unit, limit):
    best = None
    for step in range(unit, limit + 1, unit):
        if total % step == 0:
            best = step
    return best if best is not None else total


def payload_kernel(expert_count, *refs):
    inputs, rest = refs[:5], refs[5:]
    out_ref, near, sems = rest[0], rest[1:6], rest[6]
    copies = [pltpu.make_async_copy(inputs[at], near[at], sems.at[at]) for at in range(5)]
    for copy in copies:
        copy.start()
    for copy in copies:
        copy.wait()
    live_ref, tokens_ref, ids_ref, gates_ref, gain_ref = near
    step_count, row_count, width = tokens_ref.shape
    top_count = ids_ref.shape[3]
    lane = lax.broadcasted_iota(jnp.int32, (row_count, LANES), 1)
    position = lax.broadcasted_iota(jnp.int32, (row_count, LANES), 0)
    third = jnp.where(lane >= 2 * expert_count, 2, jnp.where(lane >= expert_count, 1, 0))
    named = lane - third * expert_count
    for step_at in range(step_count):
        rows = pl.ds(step_at * row_count, row_count)
        widened = tokens_ref[step_at].astype(F32)
        scaling = lax.rsqrt(jnp.sum(widened * widened, axis=-1, keepdims=True) / width + EPSILON)
        out_ref[rows, pl.ds(0, width)] = (widened * scaling * gain_ref[...]).astype(BF16)
        table = jnp.zeros((row_count, LANES), F32)
        for k in range(top_count):
            chosen = ids_ref[0, step_at, :, k : k + 1]
            gate = gates_ref[0, step_at, :, k : k + 1]
            table = table + jnp.where(named == chosen, gate, 0.0)
        table = jnp.where(position < live_ref[:, step_at : step_at + 1], table, 0.0)
        high = table.astype(BF16).astype(F32)
        rest = table - high
        middle = rest.astype(BF16).astype(F32)
        low = rest - middle
        split = jnp.where(third == 0, high, jnp.where(third == 1, middle, low))
        split = jnp.where(lane < 3 * expert_count, split, 0.0)
        out_ref[rows, pl.ds(width, LANES)] = split.astype(BF16)


def make_payload(tokens, live_rows, expert_ids, gate_weights, norm_gain, expert_count):
    step_count, row_count, width = tokens.shape
    inputs = (live_rows, tokens, expert_ids, gate_weights, norm_gain)
    return pl.pallas_call(
        functools.partial(payload_kernel, expert_count),
        out_shape=jax.ShapeDtypeStruct((step_count * row_count, width + LANES), BF16),
        in_specs=[hbm_spec()] * 5,
        out_specs=vmem_spec(),
        scratch_shapes=[pltpu.VMEM(value.shape, value.dtype) for value in inputs] + [pltpu.SemaphoreType.DMA((5,))],
        compiler_params=small_grant(),
        cost_estimate=pl.CostEstimate(flops=8 * tokens.size, bytes_accessed=6 * tokens.size, transcendentals=0),
    )(*[in_hbm(value) for value in inputs])


def join_kernel(count, height, picks, masks, first_column, *refs):
    operands, outs = refs[:count], refs[len(refs) - len(picks) :]

    def total(block, columns):
        rows = pl.ds(block * height, height)
        value = operands[0][rows, columns].astype(F32)
        for operand in operands[1:]:
            value = value + operand[rows, columns].astype(F32)
        return value

    for blocks, out_ref in zip(picks, outs, strict=True):
        for at, block in enumerate(blocks):
            out_ref[pl.ds(at * height, height), :] = total(block, slice(None)).astype(out_ref.dtype)
    if not masks:
        return
    shared_ref = refs[count]
    features, width = shared_ref.shape[2], operands[0].shape[1]
    group = lax.div(lax.axis_index("expert"), 2)
    start = group * features - first_column

    @pl.when((start >= 0) & (start < width))
    def _():
        columns = pl.ds(pl.multiple_of(start, LANES), features)
        for blocks, out_ref in zip(picks, outs, strict=True):
            for at, block in enumerate(blocks):
                value = total(block, columns) + shared_ref[jnp.bitwise_xor(group, masks[block])].astype(F32)
                out_ref[pl.ds(at * height, height), columns] = value.astype(out_ref.dtype)


def join(operands, height, picks, shared=None, masks=(), first_column=0):
    columns = operands[0].shape[1]
    size = operands[0].size
    extra = [] if shared is None else [shared]
    return list(
        pl.pallas_call(
            functools.partial(
                join_kernel, len(operands), height, picks, () if shared is None else masks, first_column
            ),
            out_shape=[
                jax.ShapeDtypeStruct((len(blocks) * height, columns), F32 if at == 0 else BF16)
                for at, blocks in enumerate(picks)
            ],
            in_specs=[vmem_spec()] * (len(operands) + len(extra)),
            out_specs=[vmem_spec()] * len(picks),
            compiler_params=small_grant(),
            cost_estimate=pl.CostEstimate(
                flops=len(operands) * size, bytes_accessed=(2 * len(operands) + 4) * size, transcendentals=0
            ),
        )(*operands, *extra)
    )


def pair_copies(own_hbm, other_hbm, weight_ref, sems):
    features = own_hbm.shape[0]
    core = lax.rem(lax.axis_index("expert"), 2)
    own_at = pl.multiple_of(core * features, 16)
    other_at = pl.multiple_of((1 - core) * features, 16)
    own = pltpu.make_async_copy(own_hbm, weight_ref.at[pl.ds(own_at, features), :], sems.at[0])
    other = pltpu.make_async_copy(other_hbm, weight_ref.at[pl.ds(other_at, features), :], sems.at[1])
    return own, other


def pair_kernel(own_hbm, other_hbm, weight_ref, sems):
    copies = pair_copies(own_hbm, other_hbm, weight_ref, sems)
    for copy in copies:
        copy.start()
    for copy in copies:
        copy.wait()


def pair_up(own, other):
    rows, columns = own.shape
    return pl.pallas_call(
        pair_kernel,
        out_shape=pltpu.VMEM((2 * rows, columns), BF16),
        in_specs=[any_spec()] * 2,
        out_specs=vmem_spec(),
        scratch_shapes=[pltpu.SemaphoreType.DMA((2,))],
        compiler_params=small_grant(),
        cost_estimate=pl.CostEstimate(flops=0, bytes_accessed=4 * rows * columns, transcendentals=0),
    )(in_hbm(own), other)


def shared_up_kernel(masks, *refs):
    blocks = refs[: len(masks)]
    weight_ref, out_ref, rows_ref = refs[len(masks) :]
    height, width = blocks[0].shape
    features = weight_ref.shape[0]
    group = lax.div(lax.axis_index("expert"), 2)
    start = 0 if width == features else pl.multiple_of(group * features, LANES)
    for at, block in enumerate(blocks):
        rows_ref[pl.ds(at * height, height), :] = block[:, pl.ds(start, features)]
    partial_value = jnp.dot(rows_ref[...], weight_ref[...], preferred_element_type=F32).astype(BF16)
    for at, mask in enumerate(masks):
        out_ref[jnp.bitwise_xor(group, mask)] = partial_value[at * height : (at + 1) * height]


def shared_up(blocks, masks, weight):
    count, height = len(blocks), blocks[0].shape[0]
    features, columns = weight.shape
    if features % LANES != 0:
        first = lax.axis_index("expert") // 2 * features
        blocks = [lax.dynamic_slice_in_dim(block, first, features, 1) for block in blocks]
    return pl.pallas_call(
        functools.partial(shared_up_kernel, masks),
        out_shape=jax.ShapeDtypeStruct((count, height, columns), BF16),
        in_specs=[vmem_spec()] * (count + 1),
        out_specs=vmem_spec(),
        scratch_shapes=[pltpu.VMEM((count * height, features), BF16)],
        compiler_params=small_grant(),
        cost_estimate=pl.CostEstimate(
            flops=2 * count * height * features * columns, bytes_accessed=2 * features * columns, transcendentals=0
        ),
    )(*blocks, weight)


def shared_down_kernel(blocks_ref, own_hbm, other_hbm, out_ref, rows_ref, weight_ref, sems):
    count, height, _ = blocks_ref.shape
    own, other = pair_copies(own_hbm, other_hbm, weight_ref, sems)
    own.start()
    other.start()
    for at in range(count):
        rows_ref[pl.ds(at * height, height), :] = blocks_ref[at]
    own.wait()
    other.wait()
    contract = (((1,), (1,)), ((), ()))
    result = lax.dot_general(rows_ref[...], weight_ref[...], contract, preferred_element_type=F32).astype(BF16)
    for at in range(count):
        out_ref[at] = result[at * height : (at + 1) * height]


def shared_down_rows(blocks, own, other):
    count, height, depth = blocks.shape
    features = 2 * own.shape[0]
    return pl.pallas_call(
        shared_down_kernel,
        out_shape=jax.ShapeDtypeStruct((count, height, features), BF16),
        in_specs=[vmem_spec()] + [any_spec()] * 2,
        out_specs=vmem_spec(),
        scratch_shapes=[
            pltpu.VMEM((count * height, depth), BF16),
            pltpu.VMEM((features, depth), BF16),
            pltpu.SemaphoreType.DMA((2,)),
        ],
        compiler_params=small_grant(),
        cost_estimate=pl.CostEstimate(
            flops=2 * count * height * depth * features, bytes_accessed=2 * depth * features, transcendentals=0
        ),
    )(blocks, in_hbm(own), other)


def shared_hidden_kernel(parts_ref, out_ref):
    count, _, columns = parts_ref.shape
    total = parts_ref[0].astype(F32)
    for at in range(1, count):
        total = total + parts_ref[at].astype(F32)
    half = columns // 2
    hidden = (jax.nn.silu(total[:, :half]) * total[:, half:]).astype(BF16)
    for at in range(count):
        out_ref[at] = hidden


def shared_hidden(parts):
    count, height, columns = parts.shape
    return pl.pallas_call(
        shared_hidden_kernel,
        out_shape=jax.ShapeDtypeStruct((count, height, columns // 2), BF16),
        in_specs=[vmem_spec()],
        out_specs=vmem_spec(),
        compiler_params=small_grant(),
        cost_estimate=pl.CostEstimate(flops=parts.size, bytes_accessed=3 * parts.size, transcendentals=height * columns),
    )(parts)


def routed_up_kernel(block_count, expert_count, step, *refs):
    blocks = refs[:block_count]
    weight_hbm, hidden_ref, gate_ref, rows_ref, total_ref, near_ref, sems = refs[block_count:]
    height = blocks[0].shape[0]
    width, double = weight_hbm.shape
    units = double // 2
    count, slots = width // step, near_ref.shape[0]

    def fetch(at):
        slot = lax.rem(at, slots)
        rows = pl.ds(pl.multiple_of(at * step, step), step)
        return pltpu.make_async_copy(weight_hbm.at[rows, :], near_ref.at[slot], sems.at[slot])

    for at in range(min(slots, count)):
        fetch(jnp.int32(at)).start()

    expert = lax.div(lax.axis_index("expert"), lax.axis_size("expert") // expert_count)
    lane = lax.broadcasted_iota(jnp.int32, (height, LANES), 1)
    mine = (lane == expert) | (lane == expert + expert_count) | (lane == expert + 2 * expert_count)
    for at, block in enumerate(blocks):
        rows = pl.ds(at * height, height)
        rows_ref[rows, :] = block[:, pl.ds(0, width)]
        table = jnp.where(mine, block[:, pl.ds(width, LANES)].astype(F32), 0.0)
        gate_ref[rows, :] = jnp.broadcast_to(jnp.sum(table, axis=1, keepdims=True), (height, LANES))
    total_ref[...] = jnp.zeros_like(total_ref)

    def body(at, carry):
        fetch(at).wait()
        columns = pl.ds(pl.multiple_of(at * step, LANES), step)
        total_ref[...] += jnp.dot(rows_ref[:, columns], near_ref[lax.rem(at, slots)], preferred_element_type=F32)

        @pl.when(at + slots < count)
        def _():
            fetch(at + slots).start()

        return carry

    lax.fori_loop(0, count, body, 0)
    hidden_ref[...] = (jax.nn.silu(total_ref[:, :units]) * total_ref[:, units:]).astype(BF16)


def routed_up(blocks, weight, expert_count):
    height = blocks[0].shape[0]
    width, double = weight.shape
    rows = len(blocks) * height
    step = largest_step(width, 2 * LANES, UP_STEP)
    return pl.pallas_call(
        functools.partial(routed_up_kernel, len(blocks), expert_count, step),
        out_shape=[jax.ShapeDtypeStruct((rows, double // 2), BF16), jax.ShapeDtypeStruct((rows, LANES), F32)],
        in_specs=[vmem_spec()] * len(blocks) + [hbm_spec()],
        out_specs=[vmem_spec()] * 2,
        scratch_shapes=[
            pltpu.VMEM((rows, width), BF16),
            pltpu.VMEM((rows, double), F32),
            pltpu.VMEM((UP_SLOTS, step, double), BF16),
            pltpu.SemaphoreType.DMA((UP_SLOTS,)),
        ],
        compiler_params=pltpu.CompilerParams(vmem_limit_bytes=ROUTED_GRANT),
        cost_estimate=pl.CostEstimate(
            flops=2 * rows * width * double, bytes_accessed=2 * width * double, transcendentals=rows * double // 2
        ),
    )(*blocks, in_hbm(weight))


def routed_down_kernel(step, part_count, hidden_ref, gate_ref, weight_hbm, *refs):
    outs = refs[: 2 * part_count]
    near_ref, sems = refs[2 * part_count :]
    half_rows = hidden_ref.shape[0] // 2
    count, slots = weight_hbm.shape[1] // step, near_ref.shape[0]

    def fetch(at):
        slot = lax.rem(at, slots)
        columns = pl.ds(pl.multiple_of(at * step, LANES), step)
        return pltpu.make_async_copy(weight_hbm.at[:, columns], near_ref.at[slot], sems.at[slot])

    for at in range(min(slots, count)):
        fetch(jnp.int32(at)).start()
    gate = gate_ref[:, :1]
    first = 0
    for part in range(part_count):
        keep_ref, send_ref = outs[2 * part], outs[2 * part + 1]
        in_part = keep_ref.shape[1] // step

        def body(at, carry, first=first, keep_ref=keep_ref, send_ref=send_ref):
            whole_at = first + at
            fetch(whole_at).wait()
            result = jnp.dot(hidden_ref[...], near_ref[lax.rem(whole_at, slots)], preferred_element_type=F32)
            weighted = (result.astype(BF16).astype(F32) * gate).astype(BF16)
            columns = pl.ds(pl.multiple_of(at * step, LANES), step)
            keep_ref[:, columns] = weighted[:half_rows]
            send_ref[:, columns] = weighted[half_rows:]

            @pl.when(whole_at + slots < count)
            def _():
                fetch(whole_at + slots).start()

            return carry

        lax.fori_loop(0, in_part, body, 0)
        first += in_part


def routed_down(hidden, gate, weight, widths):
    rows, units = hidden.shape
    width = weight.shape[1]
    step = largest_step(math.gcd(*widths), LANES, DOWN_STEP)
    return pl.pallas_call(
        functools.partial(routed_down_kernel, step, len(widths)),
        out_shape=[jax.ShapeDtypeStruct((rows // 2, columns), BF16) for columns in widths for _ in range(2)],
        in_specs=[vmem_spec()] * 2 + [hbm_spec()],
        out_specs=[vmem_spec()] * (2 * len(widths)),
        scratch_shapes=[pltpu.VMEM((DOWN_SLOTS, units, step), BF16), pltpu.SemaphoreType.DMA((DOWN_SLOTS,))],
        compiler_params=pltpu.CompilerParams(vmem_limit_bytes=ROUTED_GRANT),
        cost_estimate=pl.CostEstimate(
            flops=2 * rows * width * units, bytes_accessed=2 * width * units, transcendentals=0
        ),
    )(hidden, gate, in_hbm(weight))


def finish_kernel(counts, live_ref, tokens_ref, *refs):
    out_ref = refs[-1]
    step_count, row_count, _ = tokens_ref.shape
    used, first = 0, 0
    for count in counts:
        total = refs[used][...]
        for at in range(1, count):
            total = total + refs[used + at][...].astype(F32)
        width = total.shape[1]
        position = lax.broadcasted_iota(jnp.int32, (row_count, width), 0)
        columns = pl.ds(first, width)
        for step_at in range(step_count):
            added = total[step_at * row_count : (step_at + 1) * row_count]
            masked = jnp.where(position < live_ref[:, step_at : step_at + 1], added, 0.0)
            out_ref[step_at, :, columns] = (tokens_ref[step_at, :, columns].astype(F32) + masked).astype(BF16)
        used += count
        first += width


def finish(tokens, live_rows, lines):
    flat = [line for group in lines for line in group]
    return pl.pallas_call(
        functools.partial(finish_kernel, [len(group) for group in lines]),
        out_shape=jax.ShapeDtypeStruct(tokens.shape, BF16),
        in_specs=[vmem_spec()] * (2 + len(flat)),
        out_specs=vmem_spec(),
        compiler_params=small_grant(),
        cost_estimate=pl.CostEstimate(flops=8 * tokens.size, bytes_accessed=12 * tokens.size, transcendentals=0),
    )(live_rows, tokens, *flat)


def per_device(
    tokens,
    live_rows,
    expert_ids,
    gate_weights,
    norm_gain,
    expert_gate_up,
    expert_down,
    shared_gate_up,
    shared_down,
):
    device_count = lax.axis_size("expert")
    line_count = device_count // 4
    height = tokens.shape[0] * tokens.shape[1]
    live = jnp.swapaxes(live_rows, 0, 1)

    def swap(value, mask):
        return lax.ppermute(value, "expert", [(i, i ^ mask) for i in range(device_count)])

    def swap_line(values):
        swapped = []
        for k, value in enumerate(values, 1):
            swapped.append(swap(value, 4 * k))
        return swapped

    groups = [[first + 2 * at for at in range(device_count // 2)] for first in range(2)]

    def exchange(value):
        return lax.all_to_all(value, "expert", 0, 0, axis_index_groups=groups, tiled=True)

    own_up, own_down = shared_gate_up[0], jnp.swapaxes(shared_down[0], 0, 1)
    other_up = swap(own_up, 1)
    other_down = swap(own_down, 1)
    near_up = pair_up(own_up, other_up)
    payload = make_payload(tokens, live, expert_ids, gate_weights, norm_gain, EXPERTS)
    along = [payload] + swap_line([payload] * (line_count - 1))
    across = []
    for block in along:
        across.append(swap(block, 2))
    same = along + across
    masks = [2 * k for k in range(line_count)] + [2 * k + 1 for k in range(line_count)]
    beside = [swap(block, 1) for block in same]

    partial_value = shared_up(same, masks, near_up)
    width, features = tokens.shape[2], 2 * own_down.shape[0]
    unit = features if features % LANES == 0 else LANES
    first_width = (width // unit * FIRST_EIGHTHS + 4) // 8 * unit
    widths = [first_width, width - first_width]
    up_weight, down_weight = expert_gate_up[0, 0], expert_down[0, 0]
    up_weight, partial_value = lax.optimization_barrier((up_weight, partial_value))
    projected = exchange(partial_value)
    routed_hidden, gate = routed_up(same + beside, up_weight, EXPERTS)
    hidden = shared_hidden(projected)
    down_weight, hidden = lax.optimization_barrier((down_weight, hidden))
    spread = exchange(hidden)
    outs = routed_down(routed_hidden, gate, down_weight, widths)
    shared = shared_down_rows(spread, own_down, other_down)

    come = []
    for part in range(2):
        come.append(swap(outs[2 * part + 1], 1))
    lower, upper = list(range(line_count)), list(range(line_count, 2 * line_count))
    picks = ([lower, upper], [[k, line_count + k] for k in range(line_count)])
    joined = []
    for part in range(2):
        first = part * widths[0]
        if features % LANES == 0:
            joined.append(join([outs[2 * part], come[part]], height, picks[part], shared, masks, first))
        else:
            group = lax.axis_index("expert") // 2
            rows = shared[jnp.bitwise_xor(jnp.asarray(masks), group)].reshape(-1, features)
            wide = lax.dynamic_update_slice(
                jnp.zeros((rows.shape[0], width), BF16), rows, (0, group * features)
            )
            piece = wide[:, first : first + widths[part]]
            joined.append(join([outs[2 * part], come[part], piece], height, picks[part]))
    come_across = swap(joined[0][1], 2)
    come_along = swap_line(joined[1][1:])
    near = join([joined[0][0], come_across], height, [[k] for k in range(line_count)])
    first_lines = near[:1] + swap_line(near[1:])
    keep, send = join([joined[1][0]] + come_along, height, [[0], [1]])
    second_lines = [keep, swap(send, 2)]
    return finish(tokens, live, [first_lines, second_lines])


def solution(mesh):
    placed = (
        P(None, ("parts", "expert"), None),
        P(None, ("parts", "expert")),
        P(None, None, ("parts", "expert"), None),
        P(None, None, ("parts", "expert"), None),
        P(),
        P(None, "expert", None, None),
        P(None, "expert", None, None),
        P(None, "expert", None),
        P(None, None, "expert"),
    )
    return jax.shard_map(
        per_device,
        mesh=mesh,
        in_specs=placed,
        out_specs=P(None, ("parts", "expert"), None),
        check_vma=False,
    )
```

```python
import functools
import math

import jax
import jax.numpy as jnp
from jax import lax
from jax.experimental import pallas as pl
from jax.experimental.pallas import tpu as pltpu
from jax.sharding import PartitionSpec as P


EXPERTS = 16
EPSILON = 1e-06
LANES = 128
SMALL_GRANT = 8 << 20
FIRST_EIGHTHS = 5
ROUTED_GRANT = 40 << 20
UP_STEP, UP_SLOTS = 512, 6
DOWN_STEP, DOWN_SLOTS = 896, 8


F32 = jnp.float32
BF16 = jnp.bfloat16


def vmem_spec():
    return pl.BlockSpec(memory_space=pltpu.VMEM)


def any_spec():
    return pl.BlockSpec(memory_space=pl.ANY)


def hbm_spec():
    return pl.BlockSpec(memory_space=pltpu.HBM)


def in_hbm(value):
    return pltpu.with_memory_space_constraint(value, pltpu.HBM)


def small_grant():
    return pltpu.CompilerParams(vmem_limit_bytes=SMALL_GRANT)


def largest_step(total, unit, limit):
    best = None
    for step in range(unit, limit + 1, unit):
        if total % step == 0:
            best = step
    return best if best is not None else total


def payload_kernel(expert_count, *refs):
    inputs, rest = refs[:5], refs[5:]
    out_ref, near, sems = rest[0], rest[1:6], rest[6]
    copies = [pltpu.make_async_copy(inputs[at], near[at], sems.at[at]) for at in range(5)]
    for copy in copies:
        copy.start()
    for copy in copies:
        copy.wait()
    live_ref, tokens_ref, ids_ref, gates_ref, gain_ref = near
    step_count, row_count, width = tokens_ref.shape
    top_count = ids_ref.shape[3]
    lane = lax.broadcasted_iota(jnp.int32, (row_count, LANES), 1)
    position = lax.broadcasted_iota(jnp.int32, (row_count, LANES), 0)
    third = jnp.where(lane >= 2 * expert_count, 2, jnp.where(lane >= expert_count, 1, 0))
    named = lane - third * expert_count
    for step_at in range(step_count):
        rows = pl.ds(step_at * row_count, row_count)
        widened = tokens_ref[step_at].astype(F32)
        scaling = lax.rsqrt(jnp.sum(widened * widened, axis=-1, keepdims=True) / width + EPSILON)
        out_ref[rows, pl.ds(0, width)] = (widened * scaling * gain_ref[...]).astype(BF16)
        table = jnp.zeros((row_count, LANES), F32)
        for k in range(top_count):
            chosen = ids_ref[0, step_at, :, k : k + 1]
            gate = gates_ref[0, step_at, :, k : k + 1]
            table = table + jnp.where(named == chosen, gate, 0.0)
        table = jnp.where(position < live_ref[:, step_at : step_at + 1], table, 0.0)
        high = table.astype(BF16).astype(F32)
        rest = table - high
        middle = rest.astype(BF16).astype(F32)
        low = rest - middle
        split = jnp.where(third == 0, high, jnp.where(third == 1, middle, low))
        split = jnp.where(lane < 3 * expert_count, split, 0.0)
        out_ref[rows, pl.ds(width, LANES)] = split.astype(BF16)


def make_payload(tokens, live_rows, expert_ids, gate_weights, norm_gain, expert_count):
    step_count, row_count, width = tokens.shape
    inputs = (live_rows, tokens, expert_ids, gate_weights, norm_gain)
    return pl.pallas_call(
        functools.partial(payload_kernel, expert_count),
        out_shape=jax.ShapeDtypeStruct((step_count * row_count, width + LANES), BF16),
        in_specs=[hbm_spec()] * 5,
        out_specs=vmem_spec(),
        scratch_shapes=[pltpu.VMEM(value.shape, value.dtype) for value in inputs] + [pltpu.SemaphoreType.DMA((5,))],
        compiler_params=small_grant(),
        cost_estimate=pl.CostEstimate(flops=8 * tokens.size, bytes_accessed=6 * tokens.size, transcendentals=0),
    )(*[in_hbm(value) for value in inputs])


def join_kernel(count, height, picks, masks, first_column, *refs):
    operands, outs = refs[:count], refs[len(refs) - len(picks) :]

    def total(block, columns):
        rows = pl.ds(block * height, height)
        value = operands[0][rows, columns].astype(F32)
        for operand in operands[1:]:
            value = value + operand[rows, columns].astype(F32)
        return value

    for blocks, out_ref in zip(picks, outs, strict=True):
        for at, block in enumerate(blocks):
            out_ref[pl.ds(at * height, height), :] = total(block, slice(None)).astype(out_ref.dtype)
    if not masks:
        return
    shared_ref = refs[count]
    features, width = shared_ref.shape[2], operands[0].shape[1]
    group = lax.div(lax.axis_index("expert"), 2)
    start = group * features - first_column

    @pl.when((start >= 0) & (start < width))
    def _():
        columns = pl.ds(pl.multiple_of(start, LANES), features)
        for blocks, out_ref in zip(picks, outs, strict=True):
            for at, block in enumerate(blocks):
                value = total(block, columns) + shared_ref[jnp.bitwise_xor(group, masks[block])].astype(F32)
                out_ref[pl.ds(at * height, height), columns] = value.astype(out_ref.dtype)


def join(operands, height, picks, shared=None, masks=(), first_column=0):
    columns = operands[0].shape[1]
    size = operands[0].size
    extra = [] if shared is None else [shared]
    return list(
        pl.pallas_call(
            functools.partial(
                join_kernel, len(operands), height, picks, () if shared is None else masks, first_column
            ),
            out_shape=[
                jax.ShapeDtypeStruct((len(blocks) * height, columns), F32 if at == 0 else BF16)
                for at, blocks in enumerate(picks)
            ],
            in_specs=[vmem_spec()] * (len(operands) + len(extra)),
            out_specs=[vmem_spec()] * len(picks),
            compiler_params=small_grant(),
            cost_estimate=pl.CostEstimate(
                flops=len(operands) * size, bytes_accessed=(2 * len(operands) + 4) * size, transcendentals=0
            ),
        )(*operands, *extra)
    )


def pair_copies(own_hbm, other_hbm, weight_ref, sems):
    features = own_hbm.shape[0]
    core = lax.rem(lax.axis_index("expert"), 2)
    own_at = pl.multiple_of(core * features, 16)
    other_at = pl.multiple_of((1 - core) * features, 16)
    own = pltpu.make_async_copy(own_hbm, weight_ref.at[pl.ds(own_at, features), :], sems.at[0])
    other = pltpu.make_async_copy(other_hbm, weight_ref.at[pl.ds(other_at, features), :], sems.at[1])
    return own, other


def pair_kernel(own_hbm, other_hbm, weight_ref, sems):
    copies = pair_copies(own_hbm, other_hbm, weight_ref, sems)
    for copy in copies:
        copy.start()
    for copy in copies:
        copy.wait()


def pair_up(own, other):
    rows, columns = own.shape
    return pl.pallas_call(
        pair_kernel,
        out_shape=pltpu.VMEM((2 * rows, columns), BF16),
        in_specs=[any_spec()] * 2,
        out_specs=vmem_spec(),
        scratch_shapes=[pltpu.SemaphoreType.DMA((2,))],
        compiler_params=small_grant(),
        cost_estimate=pl.CostEstimate(flops=0, bytes_accessed=4 * rows * columns, transcendentals=0),
    )(in_hbm(own), other)


def shared_up_kernel(masks, *refs):
    blocks = refs[: len(masks)]
    weight_ref, out_ref, rows_ref = refs[len(masks) :]
    height, width = blocks[0].shape
    features = weight_ref.shape[0]
    group = lax.div(lax.axis_index("expert"), 2)
    start = 0 if width == features else pl.multiple_of(group * features, LANES)
    for at, block in enumerate(blocks):
        rows_ref[pl.ds(at * height, height), :] = block[:, pl.ds(start, features)]
    partial_value = jnp.dot(rows_ref[...], weight_ref[...], preferred_element_type=F32).astype(BF16)
    for at, mask in enumerate(masks):
        out_ref[jnp.bitwise_xor(group, mask)] = partial_value[at * height : (at + 1) * height]


def shared_up(blocks, masks, weight):
    count, height = len(blocks), blocks[0].shape[0]
    features, columns = weight.shape
    if features % LANES != 0:
        first = lax.axis_index("expert") // 2 * features
        blocks = [lax.dynamic_slice_in_dim(block, first, features, 1) for block in blocks]
    return pl.pallas_call(
        functools.partial(shared_up_kernel, masks),
        out_shape=jax.ShapeDtypeStruct((count, height, columns), BF16),
        in_specs=[vmem_spec()] * (count + 1),
        out_specs=vmem_spec(),
        scratch_shapes=[pltpu.VMEM((count * height, features), BF16)],
        compiler_params=small_grant(),
        cost_estimate=pl.CostEstimate(
            flops=2 * count * height * features * columns, bytes_accessed=2 * features * columns, transcendentals=0
        ),
    )(*blocks, weight)


def shared_down_kernel(blocks_ref, own_hbm, other_hbm, out_ref, rows_ref, weight_ref, sems):
    count, height, _ = blocks_ref.shape
    own, other = pair_copies(own_hbm, other_hbm, weight_ref, sems)
    own.start()
    other.start()
    for at in range(count):
        rows_ref[pl.ds(at * height, height), :] = blocks_ref[at]
    own.wait()
    other.wait()
    contract = (((1,), (1,)), ((), ()))
    result = lax.dot_general(rows_ref[...], weight_ref[...], contract, preferred_element_type=F32).astype(BF16)
    for at in range(count):
        out_ref[at] = result[at * height : (at + 1) * height]


def shared_down_rows(blocks, own, other):
    count, height, depth = blocks.shape
    features = 2 * own.shape[0]
    return pl.pallas_call(
        shared_down_kernel,
        out_shape=jax.ShapeDtypeStruct((count, height, features), BF16),
        in_specs=[vmem_spec()] + [any_spec()] * 2,
        out_specs=vmem_spec(),
        scratch_shapes=[
            pltpu.VMEM((count * height, depth), BF16),
            pltpu.VMEM((features, depth), BF16),
            pltpu.SemaphoreType.DMA((2,)),
        ],
        compiler_params=small_grant(),
        cost_estimate=pl.CostEstimate(
            flops=2 * count * height * depth * features, bytes_accessed=2 * depth * features, transcendentals=0
        ),
    )(blocks, in_hbm(own), other)


def shared_hidden_kernel(parts_ref, out_ref):
    count, _, columns = parts_ref.shape
    total = parts_ref[0].astype(F32)
    for at in range(1, count):
        total = total + parts_ref[at].astype(F32)
    half = columns // 2
    hidden = (jax.nn.silu(total[:, :half]) * total[:, half:]).astype(BF16)
    for at in range(count):
        out_ref[at] = hidden


def shared_hidden(parts):
    count, height, columns = parts.shape
    return pl.pallas_call(
        shared_hidden_kernel,
        out_shape=jax.ShapeDtypeStruct((count, height, columns // 2), BF16),
        in_specs=[vmem_spec()],
        out_specs=vmem_spec(),
        compiler_params=small_grant(),
        cost_estimate=pl.CostEstimate(flops=parts.size, bytes_accessed=3 * parts.size, transcendentals=height * columns),
    )(parts)


def routed_up_kernel(block_count, expert_count, step, *refs):
    blocks = refs[:block_count]
    weight_hbm, hidden_ref, gate_ref, rows_ref, total_ref, near_ref, sems = refs[block_count:]
    height = blocks[0].shape[0]
    width, double = weight_hbm.shape
    units = double // 2
    count, slots = width // step, near_ref.shape[0]

    def fetch(at):
        slot = lax.rem(at, slots)
        rows = pl.ds(pl.multiple_of(at * step, step), step)
        return pltpu.make_async_copy(weight_hbm.at[rows, :], near_ref.at[slot], sems.at[slot])

    for at in range(min(slots, count)):
        fetch(jnp.int32(at)).start()

    expert = lax.div(lax.axis_index("expert"), lax.axis_size("expert") // expert_count)
    lane = lax.broadcasted_iota(jnp.int32, (height, LANES), 1)
    mine = (lane == expert) | (lane == expert + expert_count) | (lane == expert + 2 * expert_count)
    for at, block in enumerate(blocks):
        rows = pl.ds(at * height, height)
        rows_ref[rows, :] = block[:, pl.ds(0, width)]
        table = jnp.where(mine, block[:, pl.ds(width, LANES)].astype(F32), 0.0)
        gate_ref[rows, :] = jnp.broadcast_to(jnp.sum(table, axis=1, keepdims=True), (height, LANES))
    total_ref[...] = jnp.zeros_like(total_ref)

    def body(at, carry):
        fetch(at).wait()
        columns = pl.ds(pl.multiple_of(at * step, LANES), step)
        total_ref[...] += jnp.dot(rows_ref[:, columns], near_ref[lax.rem(at, slots)], preferred_element_type=F32)

        @pl.when(at + slots < count)
        def _():
            fetch(at + slots).start()

        return carry

    lax.fori_loop(0, count, body, 0)
    hidden_ref[...] = (jax.nn.silu(total_ref[:, :units]) * total_ref[:, units:]).astype(BF16)


def routed_up(blocks, weight, expert_count):
    height = blocks[0].shape[0]
    width, double = weight.shape
    rows = len(blocks) * height
    step = largest_step(width, 2 * LANES, UP_STEP)
    return pl.pallas_call(
        functools.partial(routed_up_kernel, len(blocks), expert_count, step),
        out_shape=[jax.ShapeDtypeStruct((rows, double // 2), BF16), jax.ShapeDtypeStruct((rows, LANES), F32)],
        in_specs=[vmem_spec()] * len(blocks) + [hbm_spec()],
        out_specs=[vmem_spec()] * 2,
        scratch_shapes=[
            pltpu.VMEM((rows, width), BF16),
            pltpu.VMEM((rows, double), F32),
            pltpu.VMEM((UP_SLOTS, step, double), BF16),
            pltpu.SemaphoreType.DMA((UP_SLOTS,)),
        ],
        compiler_params=pltpu.CompilerParams(vmem_limit_bytes=ROUTED_GRANT),
        cost_estimate=pl.CostEstimate(
            flops=2 * rows * width * double, bytes_accessed=2 * width * double, transcendentals=rows * double // 2
        ),
    )(*blocks, in_hbm(weight))


def routed_down_kernel(step, part_count, hidden_ref, gate_ref, weight_hbm, *refs):
    outs = refs[: 2 * part_count]
    near_ref, sems = refs[2 * part_count :]
    half_rows = hidden_ref.shape[0] // 2
    count, slots = weight_hbm.shape[1] // step, near_ref.shape[0]

    def fetch(at):
        slot = lax.rem(at, slots)
        columns = pl.ds(pl.multiple_of(at * step, LANES), step)
        return pltpu.make_async_copy(weight_hbm.at[:, columns], near_ref.at[slot], sems.at[slot])

    for at in range(min(slots, count)):
        fetch(jnp.int32(at)).start()
    gate = gate_ref[:, :1]
    first = 0
    for part in range(part_count):
        keep_ref, send_ref = outs[2 * part], outs[2 * part + 1]
        in_part = keep_ref.shape[1] // step

        def body(at, carry, first=first, keep_ref=keep_ref, send_ref=send_ref):
            whole_at = first + at
            fetch(whole_at).wait()
            result = jnp.dot(hidden_ref[...], near_ref[lax.rem(whole_at, slots)], preferred_element_type=F32)
            weighted = (result * gate).astype(BF16)
            columns = pl.ds(pl.multiple_of(at * step, LANES), step)
            keep_ref[:, columns] = weighted[:half_rows]
            send_ref[:, columns] = weighted[half_rows:]

            @pl.when(whole_at + slots < count)
            def _():
                fetch(whole_at + slots).start()

            return carry

        lax.fori_loop(0, in_part, body, 0)
        first += in_part


def routed_down(hidden, gate, weight, widths):
    rows, units = hidden.shape
    width = weight.shape[1]
    step = largest_step(math.gcd(*widths), LANES, DOWN_STEP)
    return pl.pallas_call(
        functools.partial(routed_down_kernel, step, len(widths)),
        out_shape=[jax.ShapeDtypeStruct((rows // 2, columns), BF16) for columns in widths for _ in range(2)],
        in_specs=[vmem_spec()] * 2 + [hbm_spec()],
        out_specs=[vmem_spec()] * (2 * len(widths)),
        scratch_shapes=[pltpu.VMEM((DOWN_SLOTS, units, step), BF16), pltpu.SemaphoreType.DMA((DOWN_SLOTS,))],
        compiler_params=pltpu.CompilerParams(vmem_limit_bytes=ROUTED_GRANT),
        cost_estimate=pl.CostEstimate(
            flops=2 * rows * width * units, bytes_accessed=2 * width * units, transcendentals=0
        ),
    )(hidden, gate, in_hbm(weight))


def finish_kernel(counts, live_ref, tokens_ref, *refs):
    out_ref = refs[-1]
    step_count, row_count, _ = tokens_ref.shape
    used, first = 0, 0
    for count in counts:
        total = refs[used][...]
        for at in range(1, count):
            total = total + refs[used + at][...].astype(F32)
        width = total.shape[1]
        position = lax.broadcasted_iota(jnp.int32, (row_count, width), 0)
        columns = pl.ds(first, width)
        for step_at in range(step_count):
            added = total[step_at * row_count : (step_at + 1) * row_count]
            masked = jnp.where(position < live_ref[:, step_at : step_at + 1], added, 0.0)
            out_ref[step_at, :, columns] = (tokens_ref[step_at, :, columns].astype(F32) + masked).astype(BF16)
        used += count
        first += width


def finish(tokens, live_rows, lines):
    flat = [line for group in lines for line in group]
    return pl.pallas_call(
        functools.partial(finish_kernel, [len(group) for group in lines]),
        out_shape=jax.ShapeDtypeStruct(tokens.shape, BF16),
        in_specs=[vmem_spec()] * (2 + len(flat)),
        out_specs=vmem_spec(),
        compiler_params=small_grant(),
        cost_estimate=pl.CostEstimate(flops=8 * tokens.size, bytes_accessed=12 * tokens.size, transcendentals=0),
    )(live_rows, tokens, *flat)


def per_device(
    tokens,
    live_rows,
    expert_ids,
    gate_weights,
    norm_gain,
    expert_gate_up,
    expert_down,
    shared_gate_up,
    shared_down,
):
    device_count = lax.axis_size("expert")
    line_count = device_count // 4
    height = tokens.shape[0] * tokens.shape[1]
    live = jnp.swapaxes(live_rows, 0, 1)

    def swap(value, mask):
        return lax.ppermute(value, "expert", [(i, i ^ mask) for i in range(device_count)])

    def swap_line(values):
        swapped = []
        for k, value in enumerate(values, 1):
            swapped.append(swap(value, 4 * k))
        return swapped

    groups = [[first + 2 * at for at in range(device_count // 2)] for first in range(2)]

    def exchange(value):
        return lax.all_to_all(value, "expert", 0, 0, axis_index_groups=groups, tiled=True)

    own_up, own_down = shared_gate_up[0], jnp.swapaxes(shared_down[0], 0, 1)
    other_up = swap(own_up, 1)
    other_down = swap(own_down, 1)
    near_up = pair_up(own_up, other_up)
    payload = make_payload(tokens, live, expert_ids, gate_weights, norm_gain, EXPERTS)
    along = [payload] + swap_line([payload] * (line_count - 1))
    across = []
    for block in along:
        across.append(swap(block, 2))
    same = along + across
    masks = [2 * k for k in range(line_count)] + [2 * k + 1 for k in range(line_count)]

    partial_value = shared_up(same, masks, near_up)
    last, partial_value = lax.optimization_barrier((same[-1], partial_value))
    beside = [swap(block, 1) for block in same[:-1] + [last]]
    width, features = tokens.shape[2], 2 * own_down.shape[0]
    unit = features if features % LANES == 0 else LANES
    first_width = (width // unit * FIRST_EIGHTHS + 4) // 8 * unit
    widths = [first_width, width - first_width]
    up_weight, down_weight = expert_gate_up[0, 0], expert_down[0, 0]
    up_weight, partial_value = lax.optimization_barrier((up_weight, partial_value))
    projected = exchange(partial_value)
    routed_hidden, gate = routed_up(same + beside, up_weight, EXPERTS)
    hidden = shared_hidden(projected)
    down_weight, hidden = lax.optimization_barrier((down_weight, hidden))
    spread = exchange(hidden)
    outs = routed_down(routed_hidden, gate, down_weight, widths)
    shared = shared_down_rows(spread, own_down, other_down)

    come = []
    for part in range(2):
        come.append(swap(outs[2 * part + 1], 1))
    lower, upper = list(range(line_count)), list(range(line_count, 2 * line_count))
    picks = ([lower, upper], [[k, line_count + k] for k in range(line_count)])
    joined = []
    for part in range(2):
        first = part * widths[0]
        if features % LANES == 0:
            joined.append(join([outs[2 * part], come[part]], height, picks[part], shared, masks, first))
        else:
            group = lax.axis_index("expert") // 2
            rows = shared[jnp.bitwise_xor(jnp.asarray(masks), group)].reshape(-1, features)
            wide = lax.dynamic_update_slice(
                jnp.zeros((rows.shape[0], width), BF16), rows, (0, group * features)
            )
            piece = wide[:, first : first + widths[part]]
            joined.append(join([outs[2 * part], come[part], piece], height, picks[part]))
    come_across = swap(joined[0][1], 2)
    come_along = swap_line(joined[1][1:])
    near = join([joined[0][0], come_across], height, [[k] for k in range(line_count)])
    first_lines = near[:1] + swap_line(near[1:])
    keep, send = join([joined[1][0]] + come_along, height, [[0], [1]])
    second_lines = [keep, swap(send, 2)]
    return finish(tokens, live, [first_lines, second_lines])


def solution(mesh):
    placed = (
        P(None, ("parts", "expert"), None),
        P(None, ("parts", "expert")),
        P(None, None, ("parts", "expert"), None),
        P(None, None, ("parts", "expert"), None),
        P(),
        P(None, "expert", None, None),
        P(None, "expert", None, None),
        P(None, "expert", None),
        P(None, None, "expert"),
    )
    return jax.shard_map(
        per_device,
        mesh=mesh,
        in_specs=placed,
        out_specs=P(None, ("parts", "expert"), None),
        check_vma=False,
    )
```
